256 devices in a mesh: ctx: 64 (over z, y_lo, x), kvh: 4 (over y_hi, core).
Axes of the slice: x: 4, y: 4 (y_hi: 2, y_lo: 2; y = y_hi * 2 + y_lo), z: 8, core: 2. Of those that a mesh axis runs over, the one named last changes fastest.
Arguments:
- queries: bfloat16 [16384, 64, 128], P('ctx', 'kvh'), may hold values from -6 to 6
- keys: bfloat16 [16384, 8, 128], P(('ctx', 'kvh')), may hold values from -6 to 6
- values: bfloat16 [16384, 8, 128], P(('ctx', 'kvh')), may hold values from -6 to 6
- doc_blocks: int32 [32], replicated, may hold values from 1 to 14, 128 in all
Outputs:
- attended: bfloat16 [16384, 64, 128], P('ctx', 'kvh')
The draws below stay inside these ranges and needn't reach their ends.
Inputs may be any that keep to these rules, and one draw needn't show every extreme that they name: document i covers doc_blocks[i] * 128 tokens; the lengths sum to 16384 tokens.
All inputs are finite; a program needn't handle non-finite values.
Results may differ from the reference program's by a relative error of at most 0.004.
Values may be sent and summed in bfloat16 or wider, within the bound.
A program may use at most 64 MiB of HBM per device.

```python
import math
import jax
import jax.numpy as jnp
import numpy as np
from jax import lax

QH = 64
KVH = 8
HD = 128
BLOCK = 128
TOK_DEV = 256
TOKENS = 16384
LOOK = 7
MAXBLK = 14
NDOCS = 32
N_CTX = 64


def rough_base(key, shape):
    first = jax.random.fold_in(key, 0)
    return jnp.clip(jax.random.normal(first, shape, jnp.float32), -6.0, 6.0)


def draw_queries(key, part):
    base = rough_base(jax.random.fold_in(key, 11), (TOKENS, QH, HD))
    return base.astype(jnp.bfloat16)


def draw_keys(key, part):
    base = rough_base(jax.random.fold_in(key, 13), (TOKENS, KVH, HD))
    return base.astype(jnp.bfloat16)


def steps_of(key, extent, cuts, low, largest):
    def one(dim, parts):
        steps = jax.random.uniform(jax.random.fold_in(jax.random.fold_in(key, 6), dim), (parts,), jnp.float32, low / len(cuts), largest / len(cuts))
        return jnp.repeat(jnp.exp(steps), extent[dim] // parts).reshape((-1,) + (1,) * (len(extent) - dim - 1))

    gain = one(*cuts[0])
    for cut in cuts[1:]:
        gain = gain * one(*cut)
    return gain


def profile(count, total, limit, slope):
    portions = [(1 << 20) // math.isqrt(grade ** slope) + 1 for grade in range(2, count + 1)]
    surplus, given = total - limit - (count - 1), [1] * (count - 1)
    while surplus > 0:
        candidates = [i for i in range(count - 1) if given[i] < limit]
        pool, remaining = sum([portions[i] for i in candidates]), surplus
        for i in candidates:
            extra = min(limit - given[i], max(1, remaining * portions[i] // pool), surplus)
            given[i] = given[i] + extra
            surplus = surplus - extra
    return np.array([limit] + given)


def ragged(own_key, amount, total, most, slope):
    if amount == 2:
        one = jax.random.randint(own_key, (), max(1, total - most), min(most, total - 1) + 1)
        return jnp.stack([one, total - one])
    tallies = jnp.asarray(profile(amount, total, most, slope), jnp.int32)
    couples = (amount - 1) // 2
    source_of, receiver = tallies[1:1 + 2 * couples:2], tallies[2:2 + 2 * couples:2]
    margin = jnp.minimum(source_of - 1, most - receiver)
    passed = jax.random.randint(jax.random.fold_in(own_key, 1), (couples,), 0, 1 << 20) % (margin + 1)
    tallies = tallies.at[1:1 + 2 * couples:2].set(source_of - passed).at[2:2 + 2 * couples:2].set(receiver + passed)
    return tallies[jax.random.permutation(jax.random.fold_in(own_key, 2), amount)]


def centred(key, shape, width, most, cuts=(), kind=jnp.bfloat16):
    array = width * jax.random.normal(key, shape, jnp.float32)
    if cuts:
        array = array * steps_of(key, shape, cuts, -0.22, 0.18)
    return jnp.clip(array, -most, most).astype(kind)


def setup_inputs(seed: int = 0) -> dict:
    key_list = jax.random.split(jax.random.key(seed), 5)
    return {
        "queries": draw_queries(jax.random.fold_in(key_list[4], 71), 0),
        "keys": draw_keys(jax.random.fold_in(key_list[4], 71), 0),
        "values": centred(key_list[2], (TOKENS, KVH, HD), 1.0, 6.0, ((0, 256),)),
        "doc_blocks": ragged(key_list[3], NDOCS, TOKENS // BLOCK, MAXBLK, 2).astype(jnp.int32),
    }


def segment_of(positions, doc_ends):
    return lax.optimization_barrier(jnp.sum((doc_ends[None, :] <= positions[:, None]).astype(jnp.int32), axis=1))

def reference(queries, keys, values, doc_blocks):
    group = QH // KVH
    reach = LOOK * TOK_DEV
    span = reach + TOK_DEV
    scale = 1.0 / math.sqrt(HD)
    doc_ends = jnp.cumsum(doc_blocks, dtype=jnp.int32) * BLOCK
    positions = jnp.arange(TOKENS, dtype=jnp.int32)
    documents = segment_of(positions, doc_ends)
    padded_keys = jnp.concatenate([jnp.zeros((reach, KVH, HD), keys.dtype), keys], axis=0)
    padded_values = jnp.concatenate([jnp.zeros((reach, KVH, HD), values.dtype), values], axis=0)
    padded_docs = jnp.concatenate([jnp.full((reach,), -1, jnp.int32), documents], axis=0)

    def one_shard(index):
        start = (index * TOK_DEV).astype(jnp.int32)
        query_block = lax.dynamic_slice_in_dim(queries, start, TOK_DEV, 0).reshape(TOK_DEV, KVH, group, HD).astype(jnp.float32)
        key_block = lax.dynamic_slice_in_dim(padded_keys, start, span, 0).astype(jnp.float32)
        value_block = lax.dynamic_slice_in_dim(padded_values, start, span, 0).astype(jnp.float32)
        key_docs = lax.dynamic_slice_in_dim(padded_docs, start, span, 0)
        query_docs = lax.dynamic_slice_in_dim(documents, start, TOK_DEV, 0)
        key_pos = start - reach + jnp.arange(span, dtype=jnp.int32)
        query_pos = start + jnp.arange(TOK_DEV, dtype=jnp.int32)
        allowed = (key_docs[None, :] == query_docs[:, None]) & (key_pos[None, :] <= query_pos[:, None])
        scores = jnp.einsum('tkgd,skd->kgts', query_block, key_block) * scale
        scores = jnp.where(allowed[None, None], scores, jnp.float32(-1e+30))
        top = lax.optimization_barrier(jnp.max(scores, axis=-1))
        weights = jnp.where(allowed[None, None], jnp.exp(scores - top[..., None]), jnp.float32(0.0))
        total = lax.optimization_barrier(jnp.sum(weights, axis=-1))
        rounded = lax.optimization_barrier(weights.astype(jnp.bfloat16)).astype(jnp.float32)
        summed = jnp.einsum('kgts,skd->kgtd', rounded, value_block)
        output = (summed / total[..., None]).transpose(2, 0, 1, 3).reshape(TOK_DEV, QH, HD)
        return output.astype(jnp.bfloat16)
    shards = lax.map(one_shard, jnp.arange(N_CTX, dtype=jnp.int32))
    return shards.reshape(TOKENS, QH, HD)
```

```python
import math

import jax
import jax.numpy as jnp
from jax import lax
from jax.experimental import pallas as pl
from jax.experimental.pallas import tpu as pltpu
from jax.sharding import PartitionSpec as P

MESH = pl.DeviceIdType.MESH
NEG = -1e30
BIG = 1e30
EXP2_SCALE = math.log2(math.e) / math.sqrt(128)
NX, NYL, NZ = 4, 2, 8
BLK = 128
ONES = 16


def kernel(
    docs, q_hbm, k_hbm, v_hbm, out, q_in, kv_in, stage, cross, buf, qs, acc, top,
    in_sem, core_ssem, core_rsem, ssem, rsem,
):
    ctx = lax.axis_index("ctx")
    kvh = lax.axis_index("kvh")
    x = ctx % NX
    yl = (ctx // NX) % NYL
    z = ctx // (NX * NYL)
    yh = kvh // 2
    core = kvh % 2

    def device(x_, yl_, z_, yh_, core_):
        return (((z_ + NZ) % NZ) * (NX * NYL) + yl_ * NX + (x_ + NX) % NX, yh_ * 2 + core_)

    sibling = device(x, yl, z, yh, 1 - core)
    x_up = device(x + 1, yl, z, yh, core)
    x_down = device(x - 1, yl, z, yh, core)
    pair = device(x, 1 - yl, z, yh, core)
    other = device(x, 1 - yl, z, 1 - yh, core)
    z_up = device(x, yl, z + 1, yh, core)
    z_down = device(x, yl, z - 1, yh, core)

    barrier = pltpu.get_barrier_semaphore()
    for neighbour in (sibling, x_up, x_down, pair, other, z_up, z_down):
        pl.semaphore_signal(barrier, inc=1, device_id=neighbour, device_id_type=MESH)

    k_copy = pltpu.make_async_copy(k_hbm, kv_in.at[0], in_sem.at[0])
    v_copy = pltpu.make_async_copy(v_hbm, kv_in.at[1], in_sem.at[1])
    q_copy = pltpu.make_async_copy(q_hbm, q_in, in_sem.at[2])
    k_copy.start()
    v_copy.start()
    q_copy.start()

    for w, copy in enumerate((k_copy, v_copy)):
        copy.wait()
        heads = jnp.swapaxes(kv_in[w].astype(jnp.float32), 0, 1).astype(jnp.bfloat16)
        for g in range(4):
            for j in range(2):
                stage[g, j, w] = heads[2 * g + j]
    half = pl.ds(pl.multiple_of(core * 64, 64), 64)
    own_block, cross_block = yh, 1 - yh
    cross_group = (1 - yh) * 2 + core
    buf[0, own_block, :, :, half] = stage[kvh]
    cross[:, :, half] = stage[cross_group]

    pl.semaphore_wait(barrier, 7)

    swap_own = pltpu.make_async_remote_copy(
        src_ref=stage.at[yh * 2 + 1 - core],
        dst_ref=buf.at[0, own_block, :, :, half],
        send_sem=core_ssem.at[0],
        recv_sem=core_rsem.at[0],
        device_id=sibling,
        device_id_type=MESH,
    )
    swap_cross = pltpu.make_async_remote_copy(
        src_ref=stage.at[(1 - yh) * 2 + 1 - core],
        dst_ref=cross.at[:, :, half],
        send_sem=core_ssem.at[1],
        recv_sem=core_rsem.at[1],
        device_id=sibling,
        device_id_type=MESH,
    )
    swap_own.start()
    swap_cross.start()

    sent = []

    def push(src, slot, block, target, when=None):
        copy = pltpu.make_async_remote_copy(
            src_ref=src,
            dst_ref=buf.at[slot, block],
            send_sem=ssem.at[len(sent)],
            recv_sem=rsem.at[slot, block],
            device_id=target,
            device_id_type=MESH,
        )
        if when is None:
            copy.start()
        else:
            pl.when(when)(copy.start)
        sent.append((copy, when))

    def send(slot_from, slot_to, block, target, when=None):
        push(buf.at[slot_from, block], slot_to, block, target, when)

    def arrived(slot, block):
        pltpu.make_async_copy(
            buf.at[slot, block], buf.at[slot, block], rsem.at[slot, block]
        ).wait()

    step_up = jnp.where(x == 3, -3, 1)
    step_down = jnp.where(x == 0, 3, -1)
    relay_up = jnp.where(x == 3, 5, 1)
    relay_down = jnp.where(x == 0, 3, 7)
    crossed = jnp.where(yl == 1, 4, 9)

    swap_own.wait()
    send(0, 4, own_block, pair, yl == 0)
    send(0, 8, own_block, z_up)
    send(0, 1, own_block, x_up, x < 3)
    send(0, 3, own_block, x_down, x == 0)
    swap_cross.wait()
    push(cross, jnp.where(yl == 1, 9, 4), own_block, other)

    q_copy.wait()
    for j in range(2):
        for b in range(2):
            qs[j, pl.ds(b * 1024, 1024)] = q_in[
                b * BLK : (b + 1) * BLK, j * 8 : (j + 1) * 8, :
            ].reshape(1024, 128)

    arrived(crossed, cross_block)
    send(crossed, 0, cross_block, pair)
    send(9, 4, cross_block, z_up, yl == 0)
    send(4, 4 + step_up, cross_block, x_up, yl == 1)
    send(4, 4 + step_down, cross_block, x_down, yl == 1)
    arrived(8, own_block)
    send(8, 4, own_block, pair, yl == 1)
    send(8, 5, own_block, x_up, x == 3)
    send(8, 7, own_block, x_down, x > 0)
    arrived(0, cross_block)
    send(0, 8, cross_block, z_up)
    send(0, 1, cross_block, x_up, x < 3)
    send(0, 3, cross_block, x_down, x == 0)
    arrived(4, own_block)
    send(4, 4 + step_up, own_block, x_up)
    send(4, 4 + step_down, own_block, x_down)
    pl.when(yl == 0)(lambda: arrived(4, cross_block))
    send(4, 4 + step_up, cross_block, x_up, yl == 0)
    send(4, 4 + step_down, cross_block, x_down, yl == 0)
    arrived(8, cross_block)
    send(8, 5, cross_block, x_up, x == 3)
    send(8, 7, cross_block, x_down, x > 0)

    first = []
    for b in range(2):
        here = ctx * 2 + b
        end = jnp.int32(0)
        start = jnp.int32(0)
        for i in range(docs.shape[0]):
            end = end + docs[i]
            start = jnp.where(end <= here, end, start)
        first.append(start)

    def attend(slot, fresh):
        units = [(j, b) for j in range(2) for b in range(2)]
        kv = []
        for j in range(2):
            keys = jnp.concatenate([buf[slot, 0, j, 0], buf[slot, 1, j, 0]], axis=0)
            vals = jnp.concatenate([buf[slot, 0, j, 1], buf[slot, 1, j, 1]], axis=0)
            kv.append(
                (keys, jnp.concatenate([vals.T, jnp.ones((ONES, 2 * BLK), jnp.bfloat16)], axis=0))
            )

        def score(unit):
            j, b = unit
            return lax.dot_general(
                kv[j][0],
                qs[j, pl.ds(b * 1024, 1024), :],
                (((1,), (1,)), ((), ())),
                preferred_element_type=jnp.float32,
            )

        def soften(unit, scores):
            j, b = unit
            cols = pl.ds(b * 1024, 1024)
            parts = [scores[:BLK], scores[BLK:]]
            if fresh:
                keep = [ctx * 2 >= first[b], b == 1]
                row = lax.broadcasted_iota(jnp.int32, (BLK, 1024), 0)
                col = lax.broadcasted_iota(jnp.int32, (BLK, 1024), 1)
                parts[b] = jnp.where(row <= col // 8, parts[b], NEG)
            else:
                near = (ctx - slot) * 2
                keep = [near >= first[b], near + 1 >= first[b]]
            tops = [jnp.max(p, axis=0, keepdims=True) for p in parts]
            tops = [jnp.where(k, t, NEG) for k, t in zip(keep, tops)]
            new = jnp.maximum(tops[0], tops[1])
            fade = None
            if not fresh:
                old = top[j, :, cols]
                new = jnp.maximum(old, new)
                fade = jnp.exp2((old - new) * EXP2_SCALE)
            top[j, :, cols] = new
            weights = [
                jnp.exp2((p - jnp.where(k, new, BIG)) * EXP2_SCALE).astype(jnp.bfloat16)
                for k, p in zip(keep, parts)
            ]
            return jnp.concatenate(weights, axis=0), fade

        def add(unit, weights, fade):
            j, b = unit
            cols = pl.ds(b * 1024, 1024)
            product = lax.dot_general(
                kv[j][1], weights, (((1,), (0,)), ((), ())), preferred_element_type=jnp.float32
            )
            acc[j, :, cols] = product if fresh else acc[j, :, cols] * fade + product

        scores, waiting = score(units[0]), None
        for i, unit in enumerate(units):
            ahead = score(units[i + 1]) if i + 1 < len(units) else None
            if waiting is not None:
                add(*waiting)
            waiting = (unit, *soften(unit, scores))
            scores = ahead
        add(*waiting)

    attend(0, True)
    attend(4, False)
    for block in (own_block, cross_block):
        arrived(relay_up, block)
        send(relay_up, relay_up + step_up, block, x_up)
        arrived(relay_down, block)
        send(relay_down, relay_down + step_down, block, x_down)
    for slot in (1, 3, 5, 7, 2, 6):
        for block in (own_block, cross_block):
            pl.when(jnp.logical_and(relay_up != slot, relay_down != slot))(
                lambda: arrived(slot, block)
            )
        attend(slot, False)

    for j in range(2):
        for b in range(2):
            part = acc[j, :, pl.ds(b * 1024, 1024)]
            rows = (part[:BLK] / part[BLK : BLK + 1]).T
            out[b * BLK : (b + 1) * BLK, j * 8 : (j + 1) * 8, :] = rows.reshape(BLK, 8, 128).astype(
                jnp.bfloat16
            )
    for copy, when in sent:
        if when is None:
            copy.wait_send()
        else:
            pl.when(when)(copy.wait_send)


def body(queries, keys, values, doc_blocks):
    bf16, f32 = jnp.bfloat16, jnp.float32
    return pl.pallas_call(
        kernel,
        out_shape=jax.ShapeDtypeStruct(queries.shape, bf16),
        in_specs=[pl.BlockSpec(memory_space=pltpu.SMEM)] + [pl.BlockSpec(memory_space=pl.ANY)] * 3,
        out_specs=pl.BlockSpec(memory_space=pltpu.VMEM),
        scratch_shapes=[
            pltpu.VMEM(queries.shape, bf16),
            pltpu.VMEM((2,) + keys.shape, bf16),
            pltpu.VMEM((4, 2, 2, 64, 128), bf16),
            pltpu.VMEM((2, 2, BLK, 128), bf16),
            pltpu.VMEM((10, 2, 2, 2, BLK, 128), bf16),
            pltpu.VMEM((2, 2048, 128), bf16),
            pltpu.VMEM((2, BLK + ONES, 2048), f32),
            pltpu.VMEM((2, 1, 2048), f32),
            pltpu.SemaphoreType.DMA((3,)),
            pltpu.SemaphoreType.DMA((2,)),
            pltpu.SemaphoreType.DMA((2,)),
            pltpu.SemaphoreType.DMA((32,)),
            pltpu.SemaphoreType.DMA((10, 2)),
        ],
        compiler_params=pltpu.CompilerParams(
            collective_id=0, has_side_effects=True, vmem_limit_bytes=58 << 20
        ),
        name="gather_attend",
    )(doc_blocks, queries, keys, values)


def solution(mesh):
    in_specs = (
        P("ctx", "kvh", None),
        P(("ctx", "kvh"), None, None),
        P(("ctx", "kvh"), None, None),
        P(),
    )
    out_specs = P("ctx", "kvh", None)
    return jax.shard_map(body, mesh=mesh, in_specs=in_specs, out_specs=out_specs, check_vma=False)
```

```python
import math

import jax
import jax.numpy as jnp
from jax import lax
from jax.experimental import pallas as pl
from jax.experimental.pallas import tpu as pltpu
from jax.sharding import PartitionSpec as P

MESH = pl.DeviceIdType.MESH
NEG = -1e30
BIG = 1e30
EXP2_SCALE = math.log2(math.e) / math.sqrt(128)
NX, NYL, NZ = 4, 2, 8
BLK = 128
ONES = 16


def kernel(
    docs, q_hbm, k_hbm, v_hbm, out, q_in, kv_in, stage, cross, buf, qs, acc, top,
    in_sem, core_ssem, core_rsem, ssem, rsem,
):
    ctx = lax.axis_index("ctx")
    kvh = lax.axis_index("kvh")
    x = ctx % NX
    yl = (ctx // NX) % NYL
    z = ctx // (NX * NYL)
    yh = kvh // 2
    core = kvh % 2

    def device(x_, yl_, z_, yh_, core_):
        return (((z_ + NZ) % NZ) * (NX * NYL) + yl_ * NX + (x_ + NX) % NX, yh_ * 2 + core_)

    sibling = device(x, yl, z, yh, 1 - core)
    x_up = device(x + 1, yl, z, yh, core)
    x_down = device(x - 1, yl, z, yh, core)
    pair = device(x, 1 - yl, z, yh, core)
    other = device(x, 1 - yl, z, 1 - yh, core)
    z_up = device(x, yl, z + 1, yh, core)
    z_down = device(x, yl, z - 1, yh, core)
    across = device(x, yl, z, 1 - yh, core)
    diagonal = device(x, 1 - yl, z + 1, yh, core)
    other_up = device(x, 1 - yl, z + 1, 1 - yh, core)
    diagonal_back = device(x, 1 - yl, z - 1, yh, core)
    other_back = device(x, 1 - yl, z - 1, 1 - yh, core)

    barrier = pltpu.get_barrier_semaphore()
    greeted = jnp.int32(0)
    for neighbour, there in (
        (sibling, True), (x_up, True), (x_down, True), (pair, True), (other, True), (across, True),
        (z_up, z < NZ - 1), (diagonal, z < NZ - 1), (other_up, z < NZ - 1),
        (z_down, z > 0), (diagonal_back, z > 0), (other_back, z > 0),
    ):
        there = jnp.logical_and(there, z >= 0)
        pl.when(there)(
            lambda: pl.semaphore_signal(barrier, inc=1, device_id=neighbour, device_id_type=MESH)
        )
        greeted = greeted + jnp.where(there, 1, 0)

    k_copy = pltpu.make_async_copy(k_hbm, kv_in.at[0], in_sem.at[0])
    v_copy = pltpu.make_async_copy(v_hbm, kv_in.at[1], in_sem.at[1])
    q_copy = pltpu.make_async_copy(q_hbm, q_in, in_sem.at[2])
    k_copy.start()
    v_copy.start()
    q_copy.start()

    for w, copy in enumerate((k_copy, v_copy)):
        copy.wait()
        heads = jnp.swapaxes(kv_in[w].astype(jnp.float32), 0, 1).astype(jnp.bfloat16)
        for g in range(4):
            for j in range(2):
                stage[g, j, w] = heads[2 * g + j]
    half = pl.ds(pl.multiple_of(core * 64, 64), 64)
    own_block, cross_block = yh, 1 - yh
    cross_group = (1 - yh) * 2 + core
    buf[0, own_block, :, :, half] = stage[kvh]
    cross[:, :, half] = stage[cross_group]

    pl.semaphore_wait(barrier, greeted)

    swap_own = pltpu.make_async_remote_copy(
        src_ref=stage.at[yh * 2 + 1 - core],
        dst_ref=buf.at[0, own_block, :, :, half],
        send_sem=core_ssem.at[0],
        recv_sem=core_rsem.at[0],
        device_id=sibling,
        device_id_type=MESH,
    )
    swap_cross = pltpu.make_async_remote_copy(
        src_ref=stage.at[(1 - yh) * 2 + 1 - core],
        dst_ref=cross.at[:, :, half],
        send_sem=core_ssem.at[1],
        recv_sem=core_rsem.at[1],
        device_id=sibling,
        device_id_type=MESH,
    )
    swap_own.start()
    swap_cross.start()

    sent = []

    def push(src, slot, block, j, target, when=None):
        copy = pltpu.make_async_remote_copy(
            src_ref=src,
            dst_ref=buf.at[slot, block, j],
            send_sem=ssem.at[len(sent)],
            recv_sem=rsem.at[slot, block, j],
            device_id=target,
            device_id_type=MESH,
        )
        if when is None:
            copy.start()
        else:
            pl.when(when)(copy.start)
        sent.append((copy, when))

    def send(slot_from, slot_to, block, j, target, when=None):
        push(buf.at[slot_from, block, j], slot_to, block, j, target, when)

    def arrived(slot, block, j, when=None):
        ref = buf.at[slot, block, j]
        copy = pltpu.make_async_copy(ref, ref, rsem.at[slot, block, j])
        if when is None:
            copy.wait()
        else:
            pl.when(when)(copy.wait)

    has_near, has_far = ctx >= 4, z > 0

    step_up = jnp.where(x == 3, -3, 1)
    step_down = jnp.where(x == 0, 3, -1)
    relay_up = jnp.where(x == 3, 5, 1)
    relay_down = jnp.where(x == 0, 3, 7)

    swap_own.wait()
    def wrap(value):
        return (value + NX) % NX

    def row_slot(at, source):
        return jnp.where(source <= at, at - source, 8 + source - at)

    def near_slot(at, source):
        return 4 + at - source

    below, above, opposite = wrap(x - 1), wrap(x + 1), wrap(x + 2)
    for j in range(2):
        send(0, row_slot(above, x), own_block, j, x_up)
        send(0, row_slot(below, x), own_block, j, x_down)
    swap_cross.wait()
    inside = z < NZ - 1
    for j in range(2):
        push(cross.at[j], 0, own_block, j, across)
    for j in range(2):
        target = tuple(jnp.where(yl == 0, p, d) for p, d in zip(pair, diagonal))
        send(0, 4, own_block, j, target, jnp.logical_or(yl == 0, inside))
    for j in range(2):
        target = tuple(jnp.where(yl == 0, p, d) for p, d in zip(other, other_up))
        push(cross.at[j], 4, own_block, j, target, jnp.logical_or(yl == 0, inside))

    for slot in range(1, 8):

        @pl.when(ctx < slot)
        def _():
            buf[slot] = jnp.zeros_like(buf[slot])

    q_copy.wait()
    for j in range(2):
        for b in range(2):
            qs[j, pl.ds(b * 1024, 1024)] = q_in[
                b * BLK : (b + 1) * BLK, j * 8 : (j + 1) * 8, :
            ].reshape(1024, 128)

    def crossed(j):
        arrived(0, cross_block, j)
        send(0, 8, cross_block, j, z_up, z < NZ - 1)
        send(0, 1, cross_block, j, x_up, x < 3)
        send(0, 3, cross_block, j, x_down, x == 0)

    def near(block, j):
        arrived(4, block, j, has_near)
        send(4, 4 + step_up, block, j, x_up, has_near)
        send(4, 4 + step_down, block, j, x_down, has_near)

    def far(block, j):
        arrived(8, block, j, has_far)
        send(8, 5, block, j, x_up, jnp.logical_and(has_far, x == 3))
        send(8, 7, block, j, x_down, jnp.logical_and(has_far, x > 0))

    def relay(block, j):
        arrived(relay_up, block, j, ctx >= relay_up)
        send(relay_up, relay_up + step_up, block, j, x_up, ctx >= relay_up)
        arrived(relay_down, block, j, ctx >= relay_down)
        send(relay_down, relay_down + step_down, block, j, x_down, ctx >= relay_down)

    def across_row(slot_of, there=None):
        arrived(slot_of(x, below), own_block, 0, there)
        send(slot_of(x, below), slot_of(above, below), own_block, 0, x_up, there)
        arrived(slot_of(x, above), own_block, 1, there)
        send(slot_of(x, above), slot_of(below, above), own_block, 1, x_down, there)

    def rest_of_row(slot_of, there=None):
        arrived(slot_of(x, above), own_block, 0, there)
        arrived(slot_of(x, below), own_block, 1, there)

    def forward(source):
        for j in range(2):
            send(
                row_slot(x, source), 8 + x - source, own_block, j, z_up,
                jnp.logical_and(source > x, inside),
            )

    def forward_opposite():
        for j in range(2):
            arrived(row_slot(x, opposite), own_block, j)
        forward(opposite)

    def ready(slot):
        if slot != 4:
            there = ctx >= slot
            for j in range(2):
                passed_on = slot == near_slot(x, above if j else below)
                open_own = jnp.logical_not(jnp.logical_or(slot <= x, passed_on))
                arrived(slot, own_block, j, jnp.logical_and(there, open_own))
                late = jnp.logical_and(relay_up != slot, relay_down != slot)
                arrived(slot, cross_block, j, jnp.logical_and(there, late))

    def both(step, *arguments):
        def run():
            for j in range(2):
                step(*arguments, j)

        return run

    first = []
    for b in range(2):
        here = ctx * 2 + b
        end = jnp.int32(0)
        start = jnp.int32(0)
        for i in range(docs.shape[0]):
            end = end + docs[i]
            start = jnp.where(end <= here, end, start)
        first.append(start)

    def attend(slot, fresh, hooks=()):
        hooks = list(hooks)
        units = [(j, b) for j in range(2) for b in range(2)]
        kv = []
        for j in range(2):
            keys = jnp.concatenate([buf[slot, 0, j, 0], buf[slot, 1, j, 0]], axis=0)
            vals = jnp.concatenate([buf[slot, 0, j, 1], buf[slot, 1, j, 1]], axis=0)
            kv.append(
                (keys, jnp.concatenate([vals.T, jnp.ones((ONES, 2 * BLK), jnp.bfloat16)], axis=0))
            )

        def score(unit):
            j, b = unit
            return lax.dot_general(
                kv[j][0],
                qs[j, pl.ds(b * 1024, 1024), :],
                (((1,), (1,)), ((), ())),
                preferred_element_type=jnp.float32,
            )

        def soften(unit, scores):
            j, b = unit
            cols = pl.ds(b * 1024, 1024)
            parts = [scores[:BLK], scores[BLK:]]
            if fresh:
                keep = [ctx * 2 >= first[b], b == 1]
                row = lax.broadcasted_iota(jnp.int32, (BLK, 1024), 0)
                col = lax.broadcasted_iota(jnp.int32, (BLK, 1024), 1)
                parts[b] = jnp.where(row <= col // 8, parts[b], NEG)
            else:
                near = (ctx - slot) * 2
                keep = [near >= first[b], near + 1 >= first[b]]
            tops = [jnp.max(p, axis=0, keepdims=True) for p in parts]
            tops = [jnp.where(k, t, NEG) for k, t in zip(keep, tops)]
            new = jnp.maximum(tops[0], tops[1])
            fade = None
            if not fresh:
                old = top[j, :, cols]
                new = jnp.maximum(old, new)
                fade = jnp.exp2((old - new) * EXP2_SCALE)
            top[j, :, cols] = new
            weights = [
                jnp.exp2((p - jnp.where(k, new, BIG)) * EXP2_SCALE).astype(jnp.bfloat16)
                for k, p in zip(keep, parts)
            ]
            return jnp.concatenate(weights, axis=0), fade

        def add(unit, weights, fade):
            j, b = unit
            cols = pl.ds(b * 1024, 1024)
            product = lax.dot_general(
                kv[j][1], weights, (((1,), (0,)), ((), ())), preferred_element_type=jnp.float32
            )
            acc[j, :, cols] = product if fresh else acc[j, :, cols] * fade + product

        scores, waiting = score(units[0]), None
        for i, unit in enumerate(units):
            ahead = score(units[i + 1]) if i + 1 < len(units) else None
            if waiting is not None:
                add(*waiting)
            waiting = (unit, *soften(unit, scores))
            scores = ahead
            if i + 1 < len(units) and hooks:
                hooks.pop(0)()
        add(*waiting)
        for hook in hooks:
            hook()

    across_row(row_slot)
    both(near, own_block)()
    both(crossed)()
    both(near, cross_block)()
    rest_of_row(row_slot)
    forward(above)
    forward(below)

    def settle():
        across_row(near_slot, has_near)
        forward_opposite()

    attend(0, True, [both(far, cross_block), settle])
    attend(4, False, [lambda: None, lambda: relay(cross_block, 0), lambda: relay(cross_block, 1)])
    for slot in (1, 3, 5, 7, 2, 6):
        ready(slot)
        attend(slot, False)

    for j in range(2):
        for b in range(2):
            part = acc[j, :, pl.ds(b * 1024, 1024)]
            rows = (part[:BLK] / part[BLK : BLK + 1]).T
            out[b * BLK : (b + 1) * BLK, j * 8 : (j + 1) * 8, :] = rows.reshape(BLK, 8, 128).astype(
                jnp.bfloat16
            )
    for copy, when in sent:
        if when is None:
            copy.wait_send()
        else:
            pl.when(when)(copy.wait_send)


def body(queries, keys, values, doc_blocks):
    bf16, f32 = jnp.bfloat16, jnp.float32
    return pl.pallas_call(
        kernel,
        out_shape=jax.ShapeDtypeStruct(queries.shape, bf16),
        in_specs=[pl.BlockSpec(memory_space=pltpu.SMEM)] + [pl.BlockSpec(memory_space=pl.ANY)] * 3,
        out_specs=pl.BlockSpec(memory_space=pltpu.VMEM),
        scratch_shapes=[
            pltpu.VMEM(queries.shape, bf16),
            pltpu.VMEM((2,) + keys.shape, bf16),
            pltpu.VMEM((4, 2, 2, 64, 128), bf16),
            pltpu.VMEM((2, 2, BLK, 128), bf16),
            pltpu.VMEM((12, 2, 2, 2, BLK, 128), bf16),
            pltpu.VMEM((2, 2048, 128), bf16),
            pltpu.VMEM((2, BLK + ONES, 2048), f32),
            pltpu.VMEM((2, 1, 2048), f32),
            pltpu.SemaphoreType.DMA((3,)),
            pltpu.SemaphoreType.DMA((2,)),
            pltpu.SemaphoreType.DMA((2,)),
            pltpu.SemaphoreType.DMA((80,)),
            pltpu.SemaphoreType.DMA((12, 2, 2)),
        ],
        compiler_params=pltpu.CompilerParams(
            collective_id=0, has_side_effects=True, vmem_limit_bytes=58 << 20
        ),
        name="gather_attend",
    )(doc_blocks, queries, keys, values)


def solution(mesh):
    in_specs = (
        P("ctx", "kvh", None),
        P(("ctx", "kvh"), None, None),
        P(("ctx", "kvh"), None, None),
        P(),
    )
    out_specs = P("ctx", "kvh", None)
    return jax.shard_map(body, mesh=mesh, in_specs=in_specs, out_specs=out_specs, check_vma=False)
```

```python
import math

import jax
import jax.numpy as jnp
from jax import lax
from jax.experimental import pallas as pl
from jax.experimental.pallas import tpu as pltpu
from jax.sharding import PartitionSpec as P

MESH = pl.DeviceIdType.MESH
NEG = -1e30
BIG = 1e30
EXP2_SCALE = math.log2(math.e) / math.sqrt(128)
NX, NYL, NZ = 4, 2, 8
BLK = 128
ONES = 16


def kernel(
    docs, q_hbm, k_hbm, v_hbm, out, q_in, kv_in, stage, cross, buf, qs, acc, top,
    in_sem, core_ssem, core_rsem, ssem, rsem, plane_sem,
):
    ctx = lax.axis_index("ctx")
    kvh = lax.axis_index("kvh")
    x = ctx % NX
    yl = (ctx // NX) % NYL
    z = ctx // (NX * NYL)
    yh = kvh // 2
    core = kvh % 2

    def device(x_, yl_, z_, yh_, core_):
        return (((z_ + NZ) % NZ) * (NX * NYL) + yl_ * NX + (x_ + NX) % NX, yh_ * 2 + core_)

    sibling = device(x, yl, z, yh, 1 - core)
    x_up = device(x + 1, yl, z, yh, core)
    x_down = device(x - 1, yl, z, yh, core)
    pair = device(x, 1 - yl, z, yh, core)
    other = device(x, 1 - yl, z, 1 - yh, core)
    z_up = device(x, yl, z + 1, yh, core)
    z_down = device(x, yl, z - 1, yh, core)
    across = device(x, yl, z, 1 - yh, core)
    diagonal = device(x, 1 - yl, z + 1, yh, core)
    other_up = device(x, 1 - yl, z + 1, 1 - yh, core)
    diagonal_back = device(x, 1 - yl, z - 1, yh, core)
    other_back = device(x, 1 - yl, z - 1, 1 - yh, core)

    barrier = pltpu.get_barrier_semaphore()
    def greet(device_id, semaphore, when=None):
        def signal():
            pl.semaphore_signal(semaphore, inc=1, device_id=device_id, device_id_type=MESH)

        signal() if when is None else pl.when(when)(signal)

    inside, behind = z < NZ - 1, z > 0
    odd, even = yl == 1, yl == 0
    for neighbour in (sibling, x_up, x_down, pair, other, across):
        greet(neighbour, barrier)
    greet(z_up, barrier, inside)
    greet(diagonal, barrier, jnp.logical_and(inside, odd))
    greet(other_up, barrier, jnp.logical_and(inside, odd))

    k_copy = pltpu.make_async_copy(k_hbm, kv_in.at[0], in_sem.at[0])
    v_copy = pltpu.make_async_copy(v_hbm, kv_in.at[1], in_sem.at[1])
    q_copy = pltpu.make_async_copy(q_hbm, q_in, in_sem.at[2])
    k_copy.start()
    v_copy.start()
    q_copy.start()

    for w, copy in enumerate((k_copy, v_copy)):
        copy.wait()
        heads = jnp.swapaxes(kv_in[w].astype(jnp.float32), 0, 1).astype(jnp.bfloat16)
        for g in range(4):
            for j in range(2):
                stage[g, j, w] = heads[2 * g + j]
    half = pl.ds(pl.multiple_of(core * 64, 64), 64)
    own_block, cross_block = yh, 1 - yh
    cross_group = (1 - yh) * 2 + core
    buf[0, own_block, :, :, half] = stage[kvh]
    cross[:, :, half] = stage[cross_group]

    pl.semaphore_wait(barrier, 6 + jnp.where(behind, 1 + 2 * (1 - yl), 0))
    greet(z_down, plane_sem, behind)
    greet(diagonal_back, plane_sem, jnp.logical_and(behind, even))
    greet(other_back, plane_sem, jnp.logical_and(behind, even))

    swap_own = pltpu.make_async_remote_copy(
        src_ref=stage.at[yh * 2 + 1 - core],
        dst_ref=buf.at[0, own_block, :, :, half],
        send_sem=core_ssem.at[0],
        recv_sem=core_rsem.at[0],
        device_id=sibling,
        device_id_type=MESH,
    )
    swap_cross = pltpu.make_async_remote_copy(
        src_ref=stage.at[(1 - yh) * 2 + 1 - core],
        dst_ref=cross.at[:, :, half],
        send_sem=core_ssem.at[1],
        recv_sem=core_rsem.at[1],
        device_id=sibling,
        device_id_type=MESH,
    )
    swap_own.start()
    swap_cross.start()

    sent = []

    def push(src, slot, block, j, target, when=None):
        copy = pltpu.make_async_remote_copy(
            src_ref=src,
            dst_ref=buf.at[slot, block, j],
            send_sem=ssem.at[len(sent)],
            recv_sem=rsem.at[slot, block, j],
            device_id=target,
            device_id_type=MESH,
        )
        if when is None:
            copy.start()
        else:
            pl.when(when)(copy.start)
        sent.append((copy, when))

    def send(slot_from, slot_to, block, j, target, when=None):
        push(buf.at[slot_from, block, j], slot_to, block, j, target, when)

    def arrived(slot, block, j, when=None):
        ref = buf.at[slot, block, j]
        copy = pltpu.make_async_copy(ref, ref, rsem.at[slot, block, j])
        if when is None:
            copy.wait()
        else:
            pl.when(when)(copy.wait)

    has_near, has_far = ctx >= 4, z > 0

    step_up = jnp.where(x == 3, -3, 1)
    step_down = jnp.where(x == 0, 3, -1)
    relay_up = jnp.where(x == 3, 5, 1)
    relay_down = jnp.where(x == 0, 3, 7)

    swap_own.wait()
    def wrap(value):
        return (value + NX) % NX

    def row_slot(at, source):
        return jnp.where(source <= at, at - source, 8 + source - at)

    def near_slot(at, source):
        return 4 + at - source

    below, above, opposite = wrap(x - 1), wrap(x + 1), wrap(x + 2)
    for j in range(2):
        send(0, row_slot(above, x), own_block, j, x_up)
        send(0, row_slot(below, x), own_block, j, x_down)
    swap_cross.wait()
    for j in range(2):
        push(cross.at[j], 0, own_block, j, across)
    pl.when(jnp.logical_and(inside, odd))(lambda: pl.semaphore_wait(plane_sem, 3))
    for j in range(2):
        target = tuple(jnp.where(yl == 0, p, d) for p, d in zip(pair, diagonal))
        send(0, 4, own_block, j, target, jnp.logical_or(yl == 0, inside))
    for j in range(2):
        target = tuple(jnp.where(yl == 0, p, d) for p, d in zip(other, other_up))
        push(cross.at[j], 4, own_block, j, target, jnp.logical_or(yl == 0, inside))

    for slot in range(1, 8):

        @pl.when(ctx < slot)
        def _():
            buf[slot] = jnp.zeros_like(buf[slot])

    q_copy.wait()
    for j in range(2):
        for b in range(2):
            qs[j, pl.ds(b * 1024, 1024)] = q_in[
                b * BLK : (b + 1) * BLK, j * 8 : (j + 1) * 8, :
            ].reshape(1024, 128)

    def crossed(j):
        arrived(0, cross_block, j)
        if j == 0:
            pl.when(jnp.logical_and(inside, even))(lambda: pl.semaphore_wait(plane_sem, 1))
        send(0, 8, cross_block, j, z_up, z < NZ - 1)
        send(0, 1, cross_block, j, x_up, x < 3)
        send(0, 3, cross_block, j, x_down, x == 0)

    def near(block, j):
        arrived(4, block, j, has_near)
        send(4, 4 + step_up, block, j, x_up, has_near)
        send(4, 4 + step_down, block, j, x_down, has_near)

    def far(block, j):
        arrived(8, block, j, has_far)
        send(8, 5, block, j, x_up, jnp.logical_and(has_far, x == 3))
        send(8, 7, block, j, x_down, jnp.logical_and(has_far, x > 0))

    def relay(block, j):
        arrived(relay_up, block, j, ctx >= relay_up)
        send(relay_up, relay_up + step_up, block, j, x_up, ctx >= relay_up)
        arrived(relay_down, block, j, ctx >= relay_down)
        send(relay_down, relay_down + step_down, block, j, x_down, ctx >= relay_down)

    def across_row(slot_of, there=None):
        arrived(slot_of(x, below), own_block, 0, there)
        send(slot_of(x, below), slot_of(above, below), own_block, 0, x_up, there)
        arrived(slot_of(x, above), own_block, 1, there)
        send(slot_of(x, above), slot_of(below, above), own_block, 1, x_down, there)

    def rest_of_row(slot_of, there=None):
        arrived(slot_of(x, above), own_block, 0, there)
        arrived(slot_of(x, below), own_block, 1, there)

    def forward(source):
        for j in range(2):
            send(
                row_slot(x, source), 8 + x - source, own_block, j, z_up,
                jnp.logical_and(source > x, inside),
            )

    def forward_opposite():
        for j in range(2):
            arrived(row_slot(x, opposite), own_block, j)
        forward(opposite)

    def ready(slot):
        if slot != 4:
            there = ctx >= slot
            for j in range(2):
                passed_on = slot == near_slot(x, above if j else below)
                open_own = jnp.logical_not(jnp.logical_or(slot <= x, passed_on))
                arrived(slot, own_block, j, jnp.logical_and(there, open_own))
                late = jnp.logical_and(relay_up != slot, relay_down != slot)
                arrived(slot, cross_block, j, jnp.logical_and(there, late))

    def both(step, *arguments):
        def run():
            for j in range(2):
                step(*arguments, j)

        return run

    first = []
    for b in range(2):
        here = ctx * 2 + b
        end = jnp.int32(0)
        start = jnp.int32(0)
        for i in range(docs.shape[0]):
            end = end + docs[i]
            start = jnp.where(end <= here, end, start)
        first.append(start)

    def attend(slot, hooks=()):
        hooks = list(hooks)
        fresh = slot == 0
        units = [(j, b) for j in range(2) for b in range(2)]
        if slot == 7:
            units = [(j, 0) for j in range(2)]

        def blocks(b):
            if slot == 7:
                return (1,)
            return (0,) if fresh and b == 0 else (0, 1)

        def score(unit):
            j, b = unit
            keys = [buf[slot, e, j, 0] for e in blocks(b)]
            return lax.dot_general(
                jnp.concatenate(keys, axis=0),
                qs[j, pl.ds(b * 1024, 1024), :],
                (((1,), (1,)), ((), ())),
                preferred_element_type=jnp.float32,
            )

        def soften(unit, scores):
            j, b = unit
            cols = pl.ds(b * 1024, 1024)
            parts, keep, tops = [], [], []
            for i, e in enumerate(blocks(b)):
                part = scores[i * BLK : (i + 1) * BLK]
                if fresh and e == b:
                    row = lax.broadcasted_iota(jnp.int32, (BLK, 1024), 0)
                    col = lax.broadcasted_iota(jnp.int32, (BLK, 1024), 1)
                    part = jnp.where(row <= col // 8, part, NEG)
                parts.append(part)
                keep.append((ctx - slot) * 2 + e >= first[b])
                tops.append(jnp.where(keep[-1], jnp.max(part, axis=0, keepdims=True), NEG))
            new = tops[0] if len(tops) == 1 else jnp.maximum(tops[0], tops[1])
            fade = None
            if not fresh:
                old = top[j, :, cols]
                new = jnp.maximum(old, new)
                fade = jnp.exp2((old - new) * EXP2_SCALE)
            top[j, :, cols] = new
            weights = [
                jnp.exp2((p - jnp.where(k, new, BIG)) * EXP2_SCALE).astype(jnp.bfloat16)
                for k, p in zip(keep, parts)
            ]
            return jnp.concatenate(weights, axis=0), fade

        def add(unit, weights, fade):
            j, b = unit
            cols = pl.ds(b * 1024, 1024)
            vals = jnp.concatenate([buf[slot, e, j, 1] for e in blocks(b)], axis=0)
            ones = jnp.ones((ONES, vals.shape[0]), jnp.bfloat16)
            product = lax.dot_general(
                jnp.concatenate([vals.T, ones], axis=0), weights,
                (((1,), (0,)), ((), ())),
                preferred_element_type=jnp.float32,
            )
            acc[j, :, cols] = product if fresh else acc[j, :, cols] * fade + product

        scores, waiting = score(units[0]), None
        for i, unit in enumerate(units):
            ahead = score(units[i + 1]) if i + 1 < len(units) else None
            if waiting is not None:
                add(*waiting)
            waiting = (unit, *soften(unit, scores))
            scores = ahead
            if i + 1 < len(units) and hooks:
                hooks.pop(0)()
        add(*waiting)
        for hook in hooks:
            hook()

    across_row(row_slot)
    both(near, own_block)()
    both(crossed)()
    both(near, cross_block)()
    rest_of_row(row_slot)
    forward(above)
    forward(below)

    def settle():
        across_row(near_slot, has_near)
        forward_opposite()

    attend(0, [both(far, cross_block), settle])
    attend(4, [lambda: None, lambda: relay(cross_block, 0), lambda: relay(cross_block, 1)])
    for slot in (1, 3, 5, 7, 2, 6):
        ready(slot)
        attend(slot)

    for j in range(2):
        for b in range(2):
            part = acc[j, :, pl.ds(b * 1024, 1024)]
            rows = (part[:BLK] / part[BLK : BLK + 1]).T
            out[b * BLK : (b + 1) * BLK, j * 8 : (j + 1) * 8, :] = rows.reshape(BLK, 8, 128).astype(
                jnp.bfloat16
            )
    for copy, when in sent:
        if when is None:
            copy.wait_send()
        else:
            pl.when(when)(copy.wait_send)


def body(queries, keys, values, doc_blocks):
    bf16, f32 = jnp.bfloat16, jnp.float32
    return pl.pallas_call(
        kernel,
        out_shape=jax.ShapeDtypeStruct(queries.shape, bf16),
        in_specs=[pl.BlockSpec(memory_space=pltpu.SMEM)] + [pl.BlockSpec(memory_space=pl.ANY)] * 3,
        out_specs=pl.BlockSpec(memory_space=pltpu.VMEM),
        scratch_shapes=[
            pltpu.VMEM(queries.shape, bf16),
            pltpu.VMEM((2,) + keys.shape, bf16),
            pltpu.VMEM((4, 2, 2, 64, 128), bf16),
            pltpu.VMEM((2, 2, BLK, 128), bf16),
            pltpu.VMEM((12, 2, 2, 2, BLK, 128), bf16),
            pltpu.VMEM((2, 2048, 128), bf16),
            pltpu.VMEM((2, BLK + ONES, 2048), f32),
            pltpu.VMEM((2, 1, 2048), f32),
            pltpu.SemaphoreType.DMA((3,)),
            pltpu.SemaphoreType.DMA((2,)),
            pltpu.SemaphoreType.DMA((2,)),
            pltpu.SemaphoreType.DMA((80,)),
            pltpu.SemaphoreType.DMA((12, 2, 2)),
            pltpu.SemaphoreType.REGULAR,
        ],
        compiler_params=pltpu.CompilerParams(
            collective_id=0, has_side_effects=True, vmem_limit_bytes=58 << 20
        ),
        name="gather_attend",
    )(doc_blocks, queries, keys, values)


def solution(mesh):
    in_specs = (
        P("ctx", "kvh", None),
        P(("ctx", "kvh"), None, None),
        P(("ctx", "kvh"), None, None),
        P(),
    )
    out_specs = P("ctx", "kvh", None)
    return jax.shard_map(body, mesh=mesh, in_specs=in_specs, out_specs=out_specs, check_vma=False)
```

```python
import math

import jax
import jax.numpy as jnp
from jax import lax
from jax.experimental import pallas as pl
from jax.experimental.pallas import tpu as pltpu
from jax.sharding import PartitionSpec as P

MESH = pl.DeviceIdType.MESH
NEG = -1e30
BIG = 1e30
EXP2_SCALE = math.log2(math.e) / math.sqrt(128)
NX, NYL, NZ = 4, 2, 8
BLK = 128
ONES = 16


def kernel(
    docs, q_hbm, k_hbm, v_hbm, out, q_in, kv_in, stage, buf, qs, acc, top,
    in_sem, ssem, rsem, plane_sem,
):
    ctx = lax.axis_index("ctx")
    kvh = lax.axis_index("kvh")
    x = ctx % NX
    yl = (ctx // NX) % NYL
    z = ctx // (NX * NYL)
    yh = kvh // 2
    core = kvh % 2

    def device(x_, yl_, z_, yh_, core_):
        return (((z_ + NZ) % NZ) * (NX * NYL) + yl_ * NX + (x_ + NX) % NX, yh_ * 2 + core_)

    sibling = device(x, yl, z, yh, 1 - core)
    x_up = device(x + 1, yl, z, yh, core)
    x_down = device(x - 1, yl, z, yh, core)
    pair = device(x, 1 - yl, z, yh, core)
    other = device(x, 1 - yl, z, 1 - yh, core)
    z_up = device(x, yl, z + 1, yh, core)
    z_down = device(x, yl, z - 1, yh, core)
    across = device(x, yl, z, 1 - yh, core)
    diagonal = device(x, 1 - yl, z + 1, yh, core)
    other_up = device(x, 1 - yl, z + 1, 1 - yh, core)
    diagonal_back = device(x, 1 - yl, z - 1, yh, core)
    other_back = device(x, 1 - yl, z - 1, 1 - yh, core)

    barrier = pltpu.get_barrier_semaphore()
    def greet(device_id, semaphore, when=None):
        def signal():
            pl.semaphore_signal(semaphore, inc=1, device_id=device_id, device_id_type=MESH)

        signal() if when is None else pl.when(when)(signal)

    inside, behind = z < NZ - 1, z > 0
    odd, even = yl == 1, yl == 0
    def cores(neighbour):
        return neighbour, (neighbour[0], neighbour[1] + 1 - 2 * core)

    greet(sibling, barrier)
    for neighbour in (x_up, x_down, pair, other, across):
        for device_id in cores(neighbour):
            greet(device_id, barrier)
    greet(z_up, barrier, inside)
    for neighbour in (diagonal, other_up):
        for device_id in cores(neighbour):
            greet(device_id, barrier, jnp.logical_and(inside, odd))

    k_copy = pltpu.make_async_copy(k_hbm, kv_in.at[0], in_sem.at[0])
    v_copy = pltpu.make_async_copy(v_hbm, kv_in.at[1], in_sem.at[1])
    q_copy = pltpu.make_async_copy(q_hbm, q_in, in_sem.at[2])
    k_copy.start()
    v_copy.start()
    q_copy.start()

    for w, copy in enumerate((k_copy, v_copy)):
        copy.wait()
        heads = jnp.swapaxes(kv_in[w].astype(jnp.float32), 0, 1).astype(jnp.bfloat16)
        for g in range(4):
            for j in range(2):
                stage[g, j, w] = heads[2 * g + j]
    half = pl.ds(pl.multiple_of(core * 64, 64), 64)
    own_block, cross_block = yh, 1 - yh
    buf[0, own_block, :, :, half] = stage[kvh]

    pl.semaphore_wait(barrier, 11 + jnp.where(behind, 1 + 4 * (1 - yl), 0))
    greet(z_down, plane_sem, behind)
    for neighbour in (diagonal_back, other_back):
        for device_id in cores(neighbour):
            greet(device_id, plane_sem, jnp.logical_and(behind, even))

    sent = []

    def push(src, dst, slot, block, j, target, when=None):
        copy = pltpu.make_async_remote_copy(
            src_ref=src,
            dst_ref=dst,
            send_sem=ssem.at[len(sent)],
            recv_sem=rsem.at[slot, block, j],
            device_id=target,
            device_id_type=MESH,
        )
        if when is None:
            copy.start()
        else:
            pl.when(when)(copy.start)
        sent.append((copy, when))

    def send(slot_from, slot_to, block, j, target, when=None):
        push(
            buf.at[slot_from, block, j], buf.at[slot_to, block, j], slot_to, block, j, target, when
        )

    def send_half(slot, j, side, target, when=None):
        for c in (core, 1 - core):
            push(
                stage.at[side * 2 + c, j], buf.at[slot, own_block, j, :, half],
                slot, own_block, j, (target[0], (target[1] // 2) * 2 + c), when,
            )

    def arrived(slot, block, j, when=None):
        ref = buf.at[slot, block, j]
        copy = pltpu.make_async_copy(ref, ref, rsem.at[slot, block, j])
        if when is None:
            copy.wait()
        else:
            pl.when(when)(copy.wait)

    has_near, has_far = ctx >= 4, z > 0

    step_up = jnp.where(x == 3, -3, 1)
    step_down = jnp.where(x == 0, 3, -1)
    relay_up = jnp.where(x == 3, 5, 1)
    relay_down = jnp.where(x == 0, 3, 7)

    for j in range(2):
        push(
            stage.at[yh * 2 + 1 - core, j], buf.at[0, own_block, j, :, half],
            0, own_block, j, sibling,
        )

    def wrap(value):
        return (value + NX) % NX

    def row_slot(at, source):
        return jnp.where(source <= at, at - source, 8 + source - at)

    def near_slot(at, source):
        return 4 + at - source

    below, above, opposite = wrap(x - 1), wrap(x + 1), wrap(x + 2)
    for j in range(2):
        send_half(row_slot(above, x), j, yh, x_up)
        send_half(row_slot(below, x), j, yh, x_down)
    for j in range(2):
        send_half(0, j, 1 - yh, across)
    pl.when(jnp.logical_and(inside, odd))(lambda: pl.semaphore_wait(plane_sem, 5))
    for j in range(2):
        target = tuple(jnp.where(yl == 0, p, d) for p, d in zip(pair, diagonal))
        send_half(4, j, yh, target, jnp.logical_or(yl == 0, inside))
    for j in range(2):
        target = tuple(jnp.where(yl == 0, p, d) for p, d in zip(other, other_up))
        send_half(4, j, 1 - yh, target, jnp.logical_or(yl == 0, inside))

    for slot in range(1, 8):

        @pl.when(ctx < slot)
        def _():
            buf[slot] = jnp.zeros_like(buf[slot])

    q_copy.wait()
    for j in range(2):
        for b in range(2):
            qs[j, pl.ds(b * 1024, 1024)] = q_in[
                b * BLK : (b + 1) * BLK, j * 8 : (j + 1) * 8, :
            ].reshape(1024, 128)

    def crossed(j):
        arrived(0, cross_block, j)
        if j == 0:
            pl.when(jnp.logical_and(inside, even))(lambda: pl.semaphore_wait(plane_sem, 1))
        send(0, 8, cross_block, j, z_up, z < NZ - 1)
        send(0, 1, cross_block, j, x_up, x < 3)
        send(0, 3, cross_block, j, x_down, x == 0)

    def near(block, j):
        arrived(4, block, j, has_near)
        send(4, 4 + step_up, block, j, x_up, has_near)
        send(4, 4 + step_down, block, j, x_down, has_near)

    def far(block, j):
        arrived(8, block, j, has_far)
        send(8, 5, block, j, x_up, jnp.logical_and(has_far, x == 3))
        send(8, 7, block, j, x_down, jnp.logical_and(has_far, x > 0))

    def relay(block, j):
        arrived(relay_up, block, j, ctx >= relay_up)
        send(relay_up, relay_up + step_up, block, j, x_up, ctx >= relay_up)
        arrived(relay_down, block, j, ctx >= relay_down)
        send(relay_down, relay_down + step_down, block, j, x_down, ctx >= relay_down)

    def across_row(slot_of, there=None):
        arrived(slot_of(x, below), own_block, 0, there)
        send(slot_of(x, below), slot_of(above, below), own_block, 0, x_up, there)
        arrived(slot_of(x, above), own_block, 1, there)
        send(slot_of(x, above), slot_of(below, above), own_block, 1, x_down, there)

    def rest_of_row(slot_of, there=None):
        arrived(slot_of(x, above), own_block, 0, there)
        arrived(slot_of(x, below), own_block, 1, there)

    def forward(source):
        for j in range(2):
            send(
                row_slot(x, source), 8 + x - source, own_block, j, z_up,
                jnp.logical_and(source > x, inside),
            )

    def forward_opposite():
        for j in range(2):
            arrived(row_slot(x, opposite), own_block, j)
        forward(opposite)

    def ready(slot):
        if slot != 4:
            there = ctx >= slot
            for j in range(2):
                passed_on = slot == near_slot(x, above if j else below)
                open_own = jnp.logical_not(jnp.logical_or(slot <= x, passed_on))
                arrived(slot, own_block, j, jnp.logical_and(there, open_own))
                late = jnp.logical_and(relay_up != slot, relay_down != slot)
                arrived(slot, cross_block, j, jnp.logical_and(there, late))

    def both(step, *arguments):
        def run():
            for j in range(2):
                step(*arguments, j)

        return run

    first = []
    for b in range(2):
        here = ctx * 2 + b
        end = jnp.int32(0)
        start = jnp.int32(0)
        for i in range(docs.shape[0]):
            end = end + docs[i]
            start = jnp.where(end <= here, end, start)
        first.append(start)

    def attend(slot, hooks=()):
        hooks = list(hooks)
        fresh = slot == 0
        units = [(j, b) for j in range(2) for b in range(2)]
        if slot == 7:
            units = [(j, 0) for j in range(2)]

        def blocks(b):
            if slot == 7:
                return (1,)
            return (0,) if fresh and b == 0 else (0, 1)

        def score(unit):
            j, b = unit
            keys = [buf[slot, e, j, 0] for e in blocks(b)]
            return lax.dot_general(
                jnp.concatenate(keys, axis=0),
                qs[j, pl.ds(b * 1024, 1024), :],
                (((1,), (1,)), ((), ())),
                preferred_element_type=jnp.float32,
            )

        def soften(unit, scores):
            j, b = unit
            cols = pl.ds(b * 1024, 1024)
            parts, keep, tops = [], [], []
            for i, e in enumerate(blocks(b)):
                part = scores[i * BLK : (i + 1) * BLK]
                if fresh and e == b:
                    row = lax.broadcasted_iota(jnp.int32, (BLK, 1024), 0)
                    col = lax.broadcasted_iota(jnp.int32, (BLK, 1024), 1)
                    part = jnp.where(row <= col // 8, part, NEG)
                parts.append(part)
                keep.append((ctx - slot) * 2 + e >= first[b])
                tops.append(jnp.where(keep[-1], jnp.max(part, axis=0, keepdims=True), NEG))
            new = tops[0] if len(tops) == 1 else jnp.maximum(tops[0], tops[1])
            fade = None
            if not fresh:
                old = top[j, :, cols]
                new = jnp.maximum(old, new)
                fade = jnp.exp2((old - new) * EXP2_SCALE)
            top[j, :, cols] = new
            weights = [
                jnp.exp2((p - jnp.where(k, new, BIG)) * EXP2_SCALE).astype(jnp.bfloat16)
                for k, p in zip(keep, parts)
            ]
            return jnp.concatenate(weights, axis=0), fade

        def add(unit, weights, fade):
            j, b = unit
            cols = pl.ds(b * 1024, 1024)
            vals = jnp.concatenate([buf[slot, e, j, 1] for e in blocks(b)], axis=0)
            ones = jnp.ones((ONES, vals.shape[0]), jnp.bfloat16)
            product = lax.dot_general(
                jnp.concatenate([vals.T, ones], axis=0), weights,
                (((1,), (0,)), ((), ())),
                preferred_element_type=jnp.float32,
            )
            acc[j, :, cols] = product if fresh else acc[j, :, cols] * fade + product

        scores, waiting = score(units[0]), None
        for i, unit in enumerate(units):
            ahead = score(units[i + 1]) if i + 1 < len(units) else None
            if waiting is not None:
                add(*waiting)
            waiting = (unit, *soften(unit, scores))
            scores = ahead
            if i + 1 < len(units) and hooks:
                hooks.pop(0)()
        add(*waiting)
        for hook in hooks:
            hook()

    across_row(row_slot)
    both(near, own_block)()
    both(crossed)()
    both(near, cross_block)()
    rest_of_row(row_slot)
    forward(above)
    forward(below)

    def settle():
        across_row(near_slot, has_near)
        forward_opposite()

    for j in range(2):
        ref = buf.at[0, own_block, j, :, half]
        pltpu.make_async_copy(ref, ref, rsem.at[0, own_block, j]).wait()
    attend(0, [both(far, cross_block), settle])
    attend(4, [lambda: None, lambda: relay(cross_block, 0), lambda: relay(cross_block, 1)])
    for slot in (1, 3, 5, 7, 2, 6):
        ready(slot)
        attend(slot)

    for j in range(2):
        for b in range(2):
            part = acc[j, :, pl.ds(b * 1024, 1024)]
            rows = (part[:BLK] / part[BLK : BLK + 1]).T
            out[b * BLK : (b + 1) * BLK, j * 8 : (j + 1) * 8, :] = rows.reshape(BLK, 8, 128).astype(
                jnp.bfloat16
            )
    for copy, when in sent:
        if when is None:
            copy.wait_send()
        else:
            pl.when(when)(copy.wait_send)


def body(queries, keys, values, doc_blocks):
    bf16, f32 = jnp.bfloat16, jnp.float32
    return pl.pallas_call(
        kernel,
        out_shape=jax.ShapeDtypeStruct(queries.shape, bf16),
        in_specs=[pl.BlockSpec(memory_space=pltpu.SMEM)] + [pl.BlockSpec(memory_space=pl.ANY)] * 3,
        out_specs=pl.BlockSpec(memory_space=pltpu.VMEM),
        scratch_shapes=[
            pltpu.VMEM(queries.shape, bf16),
            pltpu.VMEM((2,) + keys.shape, bf16),
            pltpu.VMEM((4, 2, 2, 64, 128), bf16),
            pltpu.VMEM((12, 2, 2, 2, BLK, 128), bf16),
            pltpu.VMEM((2, 2048, 128), bf16),
            pltpu.VMEM((2, BLK + ONES, 2048), f32),
            pltpu.VMEM((2, 1, 2048), f32),
            pltpu.SemaphoreType.DMA((3,)),
            pltpu.SemaphoreType.DMA((80,)),
            pltpu.SemaphoreType.DMA((12, 2, 2)),
            pltpu.SemaphoreType.REGULAR,
        ],
        compiler_params=pltpu.CompilerParams(
            collective_id=0, has_side_effects=True, vmem_limit_bytes=58 << 20
        ),
        name="gather_attend",
    )(doc_blocks, queries, keys, values)


def solution(mesh):
    in_specs = (
        P("ctx", "kvh", None),
        P(("ctx", "kvh"), None, None),
        P(("ctx", "kvh"), None, None),
        P(),
    )
    out_specs = P("ctx", "kvh", None)
    return jax.shard_map(body, mesh=mesh, in_specs=in_specs, out_specs=out_specs, check_vma=False)
```
